32 devices in a mesh: mode: 8 (over z, y), tm: 4 (over x, core).
Axes of the slice: x: 2, y: 2, z: 4, core: 2. Of those that a mesh axis runs over, the one named last changes fastest.
Arguments:
- support_accel: bfloat16 [512, 2048], P(None, 'tm'), may hold values from -6 to 6
- participation: bfloat16 [2048, 512], P('mode'), may hold values from -0.25 to 0.25
- kernels: float32 [2048, 2048], P('mode'), may hold values from -0.25 to 0.25
- lengths: int32 [2048], P('mode'), may hold values from 1 to 2048, as said below
- mode_shapes: bfloat16 [16384, 2048], P('mode'), may hold values from -0.125 to 0.125
- groups: int32 [16384], P('mode'), may hold values from 0 to 511
Outputs:
- response: bfloat16 [16384, 2048], P('mode', 'tm')
The draws below stay inside these ranges and needn't reach their ends.
Inputs may be any that keep to these rules, and one draw needn't show every extreme that they name: `lengths`: some mode has exactly 2048 taps in every draw.
All inputs are finite; a program needn't handle non-finite values.
Results may differ from the reference program's by a relative error of at most 0.0033.
Values may be sent and summed in bfloat16 or wider, within the bound.
A program may use at most 64 MiB of HBM per device.

```python
import math
import jax
import jax.numpy as jnp
from jax import lax

MODES = 2048
SUPPORTS = 512
LMAX = 2048
TIME = 2048
DOFS = 16384


def draw_lengths(key, part):
    first_key = jax.random.fold_in(key, 0)
    index = jnp.arange(MODES, dtype=jnp.int32)
    remain = MODES - index
    ceiling = remain * LMAX // MODES * remain // MODES
    ceiling = jnp.maximum(ceiling, 1)
    chosen = jax.random.randint(first_key, (MODES,), 1, ceiling + 1)
    chosen = jnp.where(index == 0, LMAX, chosen)
    return chosen.astype(jnp.int32)


def place_ends(result, rng, low, high):
    spot = [jax.random.randint(jax.random.fold_in(rng, axis), (), 0, length) for axis, length in enumerate(result.shape)]
    main_axis = result.shape.index(max(result.shape))
    next_to = spot[:main_axis] + [(spot[main_axis] + 1) % result.shape[main_axis]] + spot[main_axis + 1:]
    return result.at[tuple(spot)].set(low).at[tuple(next_to)].set(high)


def level_of(rng, dims, cuts, smallest, top_value):
    level = 1.0
    for axis_at, shards_of in cuts:
        steps = jax.random.uniform(jax.random.fold_in(jax.random.fold_in(rng, 6), axis_at), (shards_of,), jnp.float32, smallest / len(cuts), top_value / len(cuts))
        level = level * jnp.repeat(jnp.exp(steps), dims[axis_at] // shards_of).reshape((-1,) + (1,) * (len(dims) - 1 - axis_at))
    return level


def centred(key, dims, deviation, reach, cuts=(), held_as=jnp.bfloat16):
    entries = deviation * jax.random.normal(key, dims, jnp.float32)
    if cuts:
        entries = entries * level_of(key, dims, cuts, -0.22, 0.18)
    return jnp.clip(entries, -reach, reach).astype(held_as)


def setup_inputs(seed: int = 0) -> dict:
    arg_keys = jax.random.split(jax.random.key(seed), 7)
    return {
        "support_accel": centred(arg_keys[0], (SUPPORTS, TIME), 1.0, 6.0, ((1, 4),)),
        "participation": centred(arg_keys[1], (MODES, SUPPORTS), SUPPORTS ** -0.5, 0.25, ((0, 8),)),
        "kernels": centred(arg_keys[2], (MODES, LMAX), (LMAX // 4) ** -0.5, 0.25, ((0, 8),), jnp.float32),
        "lengths": draw_lengths(jax.random.fold_in(arg_keys[6], 71), 0),
        "mode_shapes": centred(arg_keys[4], (DOFS, MODES), MODES ** -0.5, 0.125, ((0, 8),)),
        "groups": place_ends(jax.random.randint(arg_keys[5], (DOFS,), 0, SUPPORTS), jax.random.fold_in(arg_keys[5], 1), 0, SUPPORTS - 1).astype(jnp.int32),
    }


def reference(support_accel, participation, kernels, lengths, mode_shapes, groups):
    forces = jnp.dot(participation, support_accel, preferred_element_type=jnp.float32)
    alive = jnp.arange(LMAX, dtype=jnp.int32)[None, :] < lengths[:, None]
    masked = jnp.where(alive, kernels, jnp.zeros_like(kernels))
    length_fft = TIME + LMAX
    spectrum = jnp.fft.rfft(forces, n=length_fft, axis=1) * jnp.fft.rfft(masked, n=length_fft, axis=1)
    modal = jnp.fft.irfft(spectrum, n=length_fft, axis=1)[:, :TIME].astype(jnp.bfloat16)
    rows_block = math.gcd(DOFS, 4096)
    shaped = mode_shapes.reshape(DOFS // rows_block, rows_block, MODES)
    grouped = groups.reshape(DOFS // rows_block, rows_block)

    def expand(pair):
        shapes_block, groups_block = pair
        summed = jnp.dot(shapes_block, modal, preferred_element_type=jnp.float32)
        ground = jnp.take(support_accel, groups_block, axis=0).astype(jnp.float32)
        return (summed + ground).astype(jnp.bfloat16)

    return lax.map(expand, (shaped, grouped)).reshape(DOFS, TIME)
```

```python
import functools

import jax
import jax.numpy as jnp
import numpy as np
from jax import lax
from jax.experimental import pallas as pl
from jax.experimental.pallas import tpu as pltpu
from jax.sharding import PartitionSpec as P

BLOCK = 128
F32 = jnp.float32
BF16 = jnp.bfloat16


def split_constant(table):
    high = table.astype(BF16)
    low = (table - high.astype(np.float64)).astype(BF16)
    return high, low


def transform_tables():
    angle = np.pi * (np.arange(BLOCK)[:, None] + 0.5) / BLOCK
    time = np.arange(2 * BLOCK)[None, :]
    cos, sin = np.cos(angle * time), np.sin(angle * time)
    forward = np.concatenate([cos[:, :BLOCK], -sin[:, :BLOCK]], axis=0).T
    backward = np.concatenate([cos, -sin], axis=0) / BLOCK
    return split_constant(forward) + split_constant(backward)


def dot3(values, high, low):
    top = values.astype(BF16)
    rest = (values - top.astype(F32)).astype(BF16)
    dot = functools.partial(jnp.dot, preferred_element_type=F32)
    return dot(top, high) + (dot(rest, high) + dot(top, low))


def filter_kernel(f_ref, k_ref, len_ref, fh_ref, fl_ref, bh_ref, bl_ref, y_ref, xs, fs, hs):
    rows, times = f_ref.shape
    taps = k_ref.shape[1]
    tblocks, kblocks = times // BLOCK, taps // BLOCK
    lengths = len_ref[...]
    for c in range(kblocks):
        pos = c * BLOCK + lax.broadcasted_iota(jnp.int32, (rows, BLOCK), 1)
        part = k_ref[:, c * BLOCK:(c + 1) * BLOCK]
        xs[c * rows:(c + 1) * rows, :] = jnp.where(pos < lengths, part, jnp.zeros_like(part))
    hs[...] = dot3(xs[:kblocks * rows, :], fh_ref[...], fl_ref[...])
    for a in range(tblocks):
        xs[a * rows:(a + 1) * rows, :] = f_ref[:, a * BLOCK:(a + 1) * BLOCK]
    fs[...] = dot3(xs[:tblocks * rows, :], fh_ref[...], fl_ref[...])
    before = jnp.zeros((rows, BLOCK), F32)
    for b in range(tblocks):
        re = jnp.zeros((rows, BLOCK), F32)
        im = jnp.zeros((rows, BLOCK), F32)
        for c in range(min(b + 1, kblocks)):
            fr = fs[(b - c) * rows:(b - c + 1) * rows, :BLOCK]
            fi = fs[(b - c) * rows:(b - c + 1) * rows, BLOCK:]
            hr = hs[c * rows:(c + 1) * rows, :BLOCK]
            hi = hs[c * rows:(c + 1) * rows, BLOCK:]
            re = re + (fr * hr - fi * hi)
            im = im + (fr * hi + fi * hr)
        wide = dot3(jnp.concatenate([re, im], axis=1), bh_ref[...], bl_ref[...])
        y_ref[:, b * BLOCK:(b + 1) * BLOCK] = (before + wide[:, :BLOCK]).astype(BF16)
        before = wide[:, BLOCK:]


def filtered(forces, kernels, lengths):
    rows, times = forces.shape
    taps = kernels.shape[1]
    tables = transform_tables()
    vmem = pl.BlockSpec(memory_space=pltpu.VMEM)
    return pl.pallas_call(
        filter_kernel,
        out_shape=jax.ShapeDtypeStruct((rows, times), BF16),
        in_specs=[vmem] * 7,
        out_specs=vmem,
        scratch_shapes=[
            pltpu.VMEM((max(times, taps) // BLOCK * rows, BLOCK), F32),
            pltpu.VMEM((times // BLOCK * rows, 2 * BLOCK), F32),
            pltpu.VMEM((taps // BLOCK * rows, 2 * BLOCK), F32),
        ],
        compiler_params=pltpu.CompilerParams(vmem_limit_bytes=32 << 20),
    )(forces, kernels, lengths[:, None], *map(jnp.asarray, tables))


def recover_kernel(g_ref, s_ref, m_ref, a_ref, o_ref):
    hot = lax.broadcasted_iota(jnp.int32, (g_ref.shape[0], a_ref.shape[0]), 1) == g_ref[...]
    ground = jnp.dot(hot.astype(F32).astype(BF16), a_ref[...], preferred_element_type=F32)
    summed = jnp.dot(s_ref[...], m_ref[...], preferred_element_type=F32)
    o_ref[...] = (summed + ground).astype(BF16)


def recovered(groups, mode_shapes, modal, support_accel):
    dofs, modes = mode_shapes.shape
    supports, slab = support_accel.shape
    tile = min(256, dofs)
    return pl.pallas_call(
        recover_kernel,
        grid=(dofs // tile,),
        out_shape=jax.ShapeDtypeStruct((dofs, slab), BF16),
        in_specs=[
            pl.BlockSpec((tile, 1), lambda i: (i, 0)),
            pl.BlockSpec((tile, modes), lambda i: (i, 0)),
            pl.BlockSpec((modes, slab), lambda i: (0, 0)),
            pl.BlockSpec((supports, slab), lambda i: (0, 0)),
        ],
        out_specs=pl.BlockSpec((tile, slab), lambda i: (i, 0)),
        compiler_params=pltpu.CompilerParams(vmem_limit_bytes=60 << 20),
    )(groups[:, None], mode_shapes, modal, support_accel)


def per_device(support_accel, participation, kernels, lengths, mode_shapes, groups):
    ways = lax.axis_size("tm")
    share = kernels.shape[0] // ways
    first = lax.axis_index("tm") * share
    forces = jnp.dot(participation, support_accel, preferred_element_type=F32)
    mine = lax.all_to_all(forces, "tm", split_axis=0, concat_axis=1, tiled=True)
    modal = filtered(
        mine,
        lax.dynamic_slice_in_dim(kernels, first, share, 0),
        lax.dynamic_slice_in_dim(lengths, first, share, 0),
    )
    slab = lax.all_to_all(modal, "tm", split_axis=1, concat_axis=0, tiled=True)
    every = lax.all_gather(slab, "mode", axis=0, tiled=True)
    return recovered(groups, mode_shapes, every, support_accel)


def solution(mesh):
    placed = (
        P(None, "tm"),
        P("mode", None),
        P("mode", None),
        P("mode"),
        P("mode", None),
        P("mode"),
    )
    return jax.shard_map(
        per_device, mesh=mesh, in_specs=placed, out_specs=P("mode", "tm"), check_vma=False
    )
```

```python
import functools

import jax
import jax.numpy as jnp
import numpy as np
from jax import lax
from jax.experimental import pallas as pl
from jax.experimental.pallas import tpu as pltpu
from jax.sharding import PartitionSpec as P

BLOCK = 128
F32 = jnp.float32
BF16 = jnp.bfloat16


def split_constant(table):
    high = table.astype(BF16)
    low = (table - high.astype(np.float64)).astype(BF16)
    return high, low


def transform_tables():
    angle = np.pi * (np.arange(BLOCK)[:, None] + 0.5) / BLOCK
    time = np.arange(2 * BLOCK)[None, :]
    cos, sin = np.cos(angle * time), np.sin(angle * time)
    forward = np.concatenate([cos[:, :BLOCK], -sin[:, :BLOCK]], axis=0).T
    backward = np.concatenate([cos, -sin], axis=0) / BLOCK
    return split_constant(forward) + split_constant(backward)


def dot3(values, high, low):
    top = values.astype(BF16)
    rest = (values - top.astype(F32)).astype(BF16)
    dot = functools.partial(jnp.dot, preferred_element_type=F32)
    return dot(top, high) + (dot(rest, high) + dot(top, low))


def filter_kernel(f_ref, k_ref, len_ref, fh_ref, fl_ref, bh_ref, bl_ref, y_ref, xs, fs, hs):
    rows, times = f_ref.shape
    taps = k_ref.shape[1]
    tblocks, kblocks = times // BLOCK, taps // BLOCK
    lengths = len_ref[...]
    for c in range(kblocks):
        pos = c * BLOCK + lax.broadcasted_iota(jnp.int32, (rows, BLOCK), 1)
        part = k_ref[:, c * BLOCK:(c + 1) * BLOCK]
        xs[c * rows:(c + 1) * rows, :] = jnp.where(pos < lengths, part, jnp.zeros_like(part))
    hs[...] = dot3(xs[:kblocks * rows, :], fh_ref[...], fl_ref[...])
    for a in range(tblocks):
        xs[a * rows:(a + 1) * rows, :] = f_ref[:, a * BLOCK:(a + 1) * BLOCK]
    fs[...] = dot3(xs[:tblocks * rows, :], fh_ref[...], fl_ref[...])
    before = jnp.zeros((rows, BLOCK), F32)
    for b in range(tblocks):
        re = jnp.zeros((rows, BLOCK), F32)
        im = jnp.zeros((rows, BLOCK), F32)
        for c in range(min(b + 1, kblocks)):
            fr = fs[(b - c) * rows:(b - c + 1) * rows, :BLOCK]
            fi = fs[(b - c) * rows:(b - c + 1) * rows, BLOCK:]
            hr = hs[c * rows:(c + 1) * rows, :BLOCK]
            hi = hs[c * rows:(c + 1) * rows, BLOCK:]
            re = re + (fr * hr - fi * hi)
            im = im + (fr * hi + fi * hr)
        wide = dot3(jnp.concatenate([re, im], axis=1), bh_ref[...], bl_ref[...])
        y_ref[:, b * BLOCK:(b + 1) * BLOCK] = (before + wide[:, :BLOCK]).astype(BF16)
        before = wide[:, BLOCK:]


def filtered(forces, kernels, lengths):
    rows, times = forces.shape
    taps = kernels.shape[1]
    tables = transform_tables()
    vmem = pl.BlockSpec(memory_space=pltpu.VMEM)
    return pl.pallas_call(
        filter_kernel,
        out_shape=jax.ShapeDtypeStruct((rows, times), BF16),
        in_specs=[vmem] * 7,
        out_specs=vmem,
        scratch_shapes=[
            pltpu.VMEM((max(times, taps) // BLOCK * rows, BLOCK), F32),
            pltpu.VMEM((times // BLOCK * rows, 2 * BLOCK), F32),
            pltpu.VMEM((taps // BLOCK * rows, 2 * BLOCK), F32),
        ],
        compiler_params=pltpu.CompilerParams(vmem_limit_bytes=32 << 20),
    )(forces, kernels, lengths[:, None], *map(jnp.asarray, tables))


MESH = pl.DeviceIdType.MESH


def exchange_kernel(f_ref, o_ref, own_sem, send_sems, recv_sems):
    ways, _, slab = f_ref.shape
    i, j = lax.axis_index("mode"), lax.axis_index("tm")
    barrier = pltpu.get_barrier_semaphore()
    for d in range(1, ways):
        peer = {"mode": i, "tm": lax.rem(j + d, ways)}
        pl.semaphore_signal(barrier, inc=1, device_id=peer, device_id_type=MESH)
    pl.semaphore_wait(barrier, ways - 1)
    own = o_ref.at[:, pl.ds(pl.multiple_of(j * slab, slab), slab)]
    copies = [pltpu.make_async_copy(f_ref.at[j], own, own_sem)]
    for d in range(ways - 1, 0, -1):
        t = lax.rem(j + d, ways)
        copies.append(pltpu.make_async_remote_copy(
            f_ref.at[t], own, send_sems.at[d - 1], recv_sems.at[d - 1],
            device_id={"mode": i, "tm": t}, device_id_type=MESH,
        ))
    for copy in copies:
        copy.start()
    for copy in copies:
        copy.wait()


def exchanged(forces, ways):
    rows, slab = forces.shape
    share = rows // ways
    vmem = pl.BlockSpec(memory_space=pltpu.VMEM)
    return pl.pallas_call(
        exchange_kernel,
        out_shape=jax.ShapeDtypeStruct((share, ways * slab), forces.dtype),
        in_specs=[vmem],
        out_specs=vmem,
        scratch_shapes=[
            pltpu.SemaphoreType.DMA,
            pltpu.SemaphoreType.DMA((ways - 1,)),
            pltpu.SemaphoreType.DMA((ways - 1,)),
        ],
        compiler_params=pltpu.CompilerParams(
            collective_id=0, has_side_effects=True, vmem_limit_bytes=32 << 20
        ),
    )(forces.reshape(ways, share, slab))


def gather_kernel(ny, m_ref, o_ref, own_sem, s1, r1, s_up, r_up, s_down, r_down, s_y, r_y):
    groups, ways, _, slab = o_ref.shape
    nz = groups // ny
    i, j = lax.axis_index("mode"), lax.axis_index("tm")
    z, y = i // ny, lax.rem(i, ny)
    below, above = z > 0, z < nz - 1

    def greet(mode, tm):
        peer = {"mode": mode, "tm": tm}
        pl.semaphore_signal(barrier, inc=1, device_id=peer, device_id_type=MESH)

    barrier = pltpu.get_barrier_semaphore()
    for d in range(1, ways):
        greet(i, lax.rem(j + d, ways))
    for d in range(1, ny):
        greet(z * ny + lax.rem(y + d, ny), j)

    @pl.when(below)
    def _():
        greet(i - ny, j)

    @pl.when(above)
    def _():
        greet(i + ny, j)

    always = ways - 1 + ny - 1
    if nz == 1:
        pl.semaphore_wait(barrier, always)
    else:
        @pl.when(below & above)
        def _():
            pl.semaphore_wait(barrier, always + 2)

        @pl.when(jnp.logical_not(below & above))
        def _():
            pl.semaphore_wait(barrier, always + 1)

    mine = m_ref.at[:, pl.ds(pl.multiple_of(j * slab, slab), slab)]
    first = [pltpu.make_async_copy(mine, o_ref.at[i, j], own_sem)]
    for d in range(ways - 1, 0, -1):
        t = lax.rem(j + d, ways)
        first.append(pltpu.make_async_remote_copy(
            m_ref.at[:, pl.ds(pl.multiple_of(t * slab, slab), slab)], o_ref.at[i, j],
            s1.at[d - 1], r1.at[d - 1], device_id={"mode": i, "tm": t}, device_id_type=MESH,
        ))
    for copy in first:
        copy.start()
    for copy in first:
        copy.wait()

    def move(block, send, recv, mode):
        return pltpu.make_async_remote_copy(
            o_ref.at[block], o_ref.at[block], send, recv,
            device_id={"mode": mode, "tm": j}, device_id_type=MESH,
        )

    def up(step, block):
        return move(block, s_up.at[step], r_up.at[step], i + ny)

    def down(step, block):
        return move(block, s_down.at[step], r_down.at[step], i - ny)

    def across(slot, line, column, d):
        return move(line * ny + column, s_y.at[slot, d - 1], r_y.at[slot, d - 1], z * ny + lax.rem(y + d, ny))

    def across_start(slot, line):
        for d in range(1, ny):
            across(slot, line, y, d).start()

    def across_wait(slot, line):
        for d in range(1, ny):
            across(slot, line, y, d).wait_send()
            across(slot, line, lax.rem(y + ny - d, ny), d).wait_recv()

    @pl.when(above)
    def _():
        up(0, i).start()

    @pl.when(below)
    def _():
        down(0, i).start()

    across_start(0, z)
    for step in range(nz - 1):
        @pl.when(z - 1 - step >= 0)
        def _(step=step):
            block = i - (1 + step) * ny
            move(block, s_up.at[step], r_up.at[step], i - ny).wait_recv()
            if step + 1 < nz - 1:
                @pl.when(above)
                def _():
                    up(step + 1, block).start()
            across_start(1 + 2 * step, z - 1 - step)

        @pl.when(z + 1 + step <= nz - 1)
        def _(step=step):
            block = i + (1 + step) * ny
            move(block, s_down.at[step], r_down.at[step], i + ny).wait_recv()
            if step + 1 < nz - 1:
                @pl.when(below)
                def _():
                    down(step + 1, block).start()
            across_start(2 + 2 * step, z + 1 + step)

    across_wait(0, z)
    for step in range(nz - 1):
        @pl.when((z - step >= 0) & above)
        def _(step=step):
            up(step, i - step * ny).wait_send()

        @pl.when((z + step <= nz - 1) & below)
        def _(step=step):
            down(step, i + step * ny).wait_send()

        @pl.when(z - 1 - step >= 0)
        def _(step=step):
            across_wait(1 + 2 * step, z - 1 - step)

        @pl.when(z + 1 + step <= nz - 1)
        def _(step=step):
            across_wait(2 + 2 * step, z + 1 + step)


def gathered(modal, groups, ways):
    share, times = modal.shape
    slab = times // ways
    ny = max(ways // 2, 1)
    if groups % ny:
        ny = 1
    nz = groups // ny
    vmem = pl.BlockSpec(memory_space=pltpu.VMEM)
    dma = pltpu.SemaphoreType.DMA
    steps, others = max(nz - 1, 1), max(ny - 1, 1)
    every = pl.pallas_call(
        functools.partial(gather_kernel, ny),
        out_shape=jax.ShapeDtypeStruct((groups, ways, share, slab), modal.dtype),
        in_specs=[vmem],
        out_specs=vmem,
        scratch_shapes=[
            dma, dma((ways - 1,)), dma((ways - 1,)),
            dma((steps,)), dma((steps,)), dma((steps,)), dma((steps,)),
            dma((1 + 2 * steps, others)), dma((1 + 2 * steps, others)),
        ],
        compiler_params=pltpu.CompilerParams(
            collective_id=1, has_side_effects=True, vmem_limit_bytes=32 << 20
        ),
    )(modal)
    return every.reshape(groups * ways * share, slab)


def recover_kernel(g_ref, s_ref, m_ref, a_ref, o_ref):
    hot = lax.broadcasted_iota(jnp.int32, (g_ref.shape[0], a_ref.shape[0]), 1) == g_ref[...]
    ground = jnp.dot(hot.astype(F32).astype(BF16), a_ref[...], preferred_element_type=F32)
    summed = jnp.dot(s_ref[...], m_ref[...], preferred_element_type=F32)
    o_ref[...] = (summed + ground).astype(BF16)


def recovered(groups, mode_shapes, modal, support_accel):
    dofs, modes = mode_shapes.shape
    supports, slab = support_accel.shape
    tile = min(256, dofs)
    return pl.pallas_call(
        recover_kernel,
        grid=(dofs // tile,),
        out_shape=jax.ShapeDtypeStruct((dofs, slab), BF16),
        in_specs=[
            pl.BlockSpec((tile, 1), lambda i: (i, 0)),
            pl.BlockSpec((tile, modes), lambda i: (i, 0)),
            pl.BlockSpec((modes, slab), lambda i: (0, 0)),
            pl.BlockSpec((supports, slab), lambda i: (0, 0)),
        ],
        out_specs=pl.BlockSpec((tile, slab), lambda i: (i, 0)),
        compiler_params=pltpu.CompilerParams(vmem_limit_bytes=60 << 20),
    )(groups[:, None], mode_shapes, modal, support_accel)


def per_device(support_accel, participation, kernels, lengths, mode_shapes, groups):
    ways = lax.axis_size("tm")
    share = kernels.shape[0] // ways
    first = lax.axis_index("tm") * share
    forces = jnp.dot(participation, support_accel, preferred_element_type=F32)
    mine = exchanged(forces, ways)
    modal = filtered(
        mine,
        lax.dynamic_slice_in_dim(kernels, first, share, 0),
        lax.dynamic_slice_in_dim(lengths, first, share, 0),
    )
    every = gathered(modal, lax.axis_size("mode"), ways)
    return recovered(groups, mode_shapes, every, support_accel)


def solution(mesh):
    placed = (
        P(None, "tm"),
        P("mode", None),
        P("mode", None),
        P("mode"),
        P("mode", None),
        P("mode"),
    )
    return jax.shard_map(
        per_device, mesh=mesh, in_specs=placed, out_specs=P("mode", "tm"), check_vma=False
    )
```

```python
import functools

import jax
import jax.numpy as jnp
import numpy as np
from jax import lax
from jax.experimental import pallas as pl
from jax.experimental.pallas import tpu as pltpu
from jax.sharding import PartitionSpec as P

BLOCK = 128
F32 = jnp.float32
BF16 = jnp.bfloat16


def split_constant(table):
    high = table.astype(BF16)
    low = (table - high.astype(np.float64)).astype(BF16)
    return high, low


def transform_tables():
    angle = np.pi * (np.arange(BLOCK)[:, None] + 0.5) / BLOCK
    time = np.arange(2 * BLOCK)[None, :]
    cos, sin = np.cos(angle * time), np.sin(angle * time)
    forward = np.concatenate([cos[:, :BLOCK], -sin[:, :BLOCK]], axis=0).T
    backward = np.concatenate([cos, -sin], axis=0) / BLOCK
    return split_constant(forward) + split_constant(backward)


def dot3(values, high, low):
    top = values.astype(BF16)
    rest = (values - top.astype(F32)).astype(BF16)
    dot = functools.partial(jnp.dot, preferred_element_type=F32)
    return dot(top, high) + (dot(rest, high) + dot(top, low))


def filter_kernel(f_ref, k_ref, len_ref, fh_ref, fl_ref, bh_ref, bl_ref, y_ref, xs, fs, hs):
    rows, times = f_ref.shape
    taps = k_ref.shape[1]
    tblocks, kblocks = times // BLOCK, taps // BLOCK
    lengths = len_ref[...]
    for c in range(kblocks):
        pos = c * BLOCK + lax.broadcasted_iota(jnp.int32, (rows, BLOCK), 1)
        part = k_ref[:, c * BLOCK:(c + 1) * BLOCK]
        xs[c * rows:(c + 1) * rows, :] = jnp.where(pos < lengths, part, jnp.zeros_like(part))
    hs[...] = dot3(xs[:kblocks * rows, :], fh_ref[...], fl_ref[...])
    for a in range(tblocks):
        xs[a * rows:(a + 1) * rows, :] = f_ref[:, a * BLOCK:(a + 1) * BLOCK]
    fs[...] = dot3(xs[:tblocks * rows, :], fh_ref[...], fl_ref[...])
    before = jnp.zeros((rows, BLOCK), F32)
    for b in range(tblocks):
        re = jnp.zeros((rows, BLOCK), F32)
        im = jnp.zeros((rows, BLOCK), F32)
        for c in range(min(b + 1, kblocks)):
            fr = fs[(b - c) * rows:(b - c + 1) * rows, :BLOCK]
            fi = fs[(b - c) * rows:(b - c + 1) * rows, BLOCK:]
            hr = hs[c * rows:(c + 1) * rows, :BLOCK]
            hi = hs[c * rows:(c + 1) * rows, BLOCK:]
            re = re + (fr * hr - fi * hi)
            im = im + (fr * hi + fi * hr)
        wide = dot3(jnp.concatenate([re, im], axis=1), bh_ref[...], bl_ref[...])
        y_ref[:, b * BLOCK:(b + 1) * BLOCK] = (before + wide[:, :BLOCK]).astype(BF16)
        before = wide[:, BLOCK:]


def filtered(forces, kernels, lengths):
    rows, times = forces.shape
    taps = kernels.shape[1]
    tables = transform_tables()
    vmem = pl.BlockSpec(memory_space=pltpu.VMEM)
    return pl.pallas_call(
        filter_kernel,
        out_shape=jax.ShapeDtypeStruct((rows, times), BF16),
        in_specs=[vmem] * 7,
        out_specs=vmem,
        scratch_shapes=[
            pltpu.VMEM((max(times, taps) // BLOCK * rows, BLOCK), F32),
            pltpu.VMEM((times // BLOCK * rows, 2 * BLOCK), F32),
            pltpu.VMEM((taps // BLOCK * rows, 2 * BLOCK), F32),
        ],
        compiler_params=pltpu.CompilerParams(vmem_limit_bytes=32 << 20),
    )(forces, kernels, lengths[:, None], *map(jnp.asarray, tables))


MESH = pl.DeviceIdType.MESH


def exchange_kernel(f_ref, o_ref, own_sem, send_sems, recv_sems):
    ways, _, slab = f_ref.shape
    i, j = lax.axis_index("mode"), lax.axis_index("tm")
    barrier = pltpu.get_barrier_semaphore()
    for d in range(1, ways):
        peer = {"mode": i, "tm": lax.rem(j + d, ways)}
        pl.semaphore_signal(barrier, inc=1, device_id=peer, device_id_type=MESH)
    pl.semaphore_wait(barrier, ways - 1)
    own = o_ref.at[:, pl.ds(pl.multiple_of(j * slab, slab), slab)]
    copies = [pltpu.make_async_copy(f_ref.at[j], own, own_sem)]
    for d in range(ways - 1, 0, -1):
        t = lax.rem(j + d, ways)
        copies.append(pltpu.make_async_remote_copy(
            f_ref.at[t], own, send_sems.at[d - 1], recv_sems.at[d - 1],
            device_id={"mode": i, "tm": t}, device_id_type=MESH,
        ))
    for copy in copies:
        copy.start()
    for copy in copies:
        copy.wait()


def exchanged(forces, ways):
    rows, slab = forces.shape
    share = rows // ways
    vmem = pl.BlockSpec(memory_space=pltpu.VMEM)
    return pl.pallas_call(
        exchange_kernel,
        out_shape=jax.ShapeDtypeStruct((share, ways * slab), forces.dtype),
        in_specs=[vmem],
        out_specs=vmem,
        scratch_shapes=[
            pltpu.SemaphoreType.DMA,
            pltpu.SemaphoreType.DMA((ways - 1,)),
            pltpu.SemaphoreType.DMA((ways - 1,)),
        ],
        compiler_params=pltpu.CompilerParams(
            collective_id=0, has_side_effects=True, vmem_limit_bytes=32 << 20
        ),
    )(forces.reshape(ways, share, slab))


def gather_kernel(ny, m_ref, o_ref, own_sem, s1, r1, s_up, r_up, s_down, r_down, s_y, r_y):
    groups, ways, _, slab = o_ref.shape
    nz = groups // ny
    i, j = lax.axis_index("mode"), lax.axis_index("tm")
    z, y = i // ny, lax.rem(i, ny)
    below, above = z > 0, z < nz - 1

    def greet(mode, tm):
        peer = {"mode": mode, "tm": tm}
        pl.semaphore_signal(barrier, inc=1, device_id=peer, device_id_type=MESH)

    barrier = pltpu.get_barrier_semaphore()
    for d in range(1, ways):
        greet(i, lax.rem(j + d, ways))
    for d in range(1, ny):
        greet(z * ny + lax.rem(y + d, ny), j)

    @pl.when(below)
    def _():
        greet(i - ny, j)

    @pl.when(above)
    def _():
        greet(i + ny, j)

    always = ways - 1 + ny - 1
    if nz == 1:
        pl.semaphore_wait(barrier, always)
    else:
        @pl.when(below & above)
        def _():
            pl.semaphore_wait(barrier, always + 2)

        @pl.when(jnp.logical_not(below & above))
        def _():
            pl.semaphore_wait(barrier, always + 1)

    mine = m_ref.at[:, pl.ds(pl.multiple_of(j * slab, slab), slab)]
    first = [pltpu.make_async_copy(mine, o_ref.at[i, j], own_sem)]
    for d in range(ways - 1, 0, -1):
        t = lax.rem(j + d, ways)
        first.append(pltpu.make_async_remote_copy(
            m_ref.at[:, pl.ds(pl.multiple_of(t * slab, slab), slab)], o_ref.at[i, j],
            s1.at[d - 1], r1.at[d - 1], device_id={"mode": i, "tm": t}, device_id_type=MESH,
        ))
    for copy in first:
        copy.start()
    for copy in first:
        copy.wait()

    def move(block, send, recv, mode):
        return pltpu.make_async_remote_copy(
            o_ref.at[block], o_ref.at[block], send, recv,
            device_id={"mode": mode, "tm": j}, device_id_type=MESH,
        )

    def up(step, block):
        return move(block, s_up.at[step], r_up.at[step], i + ny)

    def down(step, block):
        return move(block, s_down.at[step], r_down.at[step], i - ny)

    def across(slot, line, column, d):
        return move(line * ny + column, s_y.at[slot, d - 1], r_y.at[slot, d - 1], z * ny + lax.rem(y + d, ny))

    def across_start(slot, line):
        for d in range(1, ny):
            across(slot, line, y, d).start()

    def across_wait(slot, line):
        for d in range(1, ny):
            across(slot, line, y, d).wait_send()
            across(slot, line, lax.rem(y + ny - d, ny), d).wait_recv()

    @pl.when(above)
    def _():
        up(0, i).start()

    @pl.when(below)
    def _():
        down(0, i).start()

    across_start(0, z)
    for step in range(nz - 1):
        @pl.when(z - 1 - step >= 0)
        def _(step=step):
            block = i - (1 + step) * ny
            move(block, s_up.at[step], r_up.at[step], i - ny).wait_recv()
            if step + 1 < nz - 1:
                @pl.when(above)
                def _():
                    up(step + 1, block).start()
            across_start(1 + 2 * step, z - 1 - step)

        @pl.when(z + 1 + step <= nz - 1)
        def _(step=step):
            block = i + (1 + step) * ny
            move(block, s_down.at[step], r_down.at[step], i + ny).wait_recv()
            if step + 1 < nz - 1:
                @pl.when(below)
                def _():
                    down(step + 1, block).start()
            across_start(2 + 2 * step, z + 1 + step)

    across_wait(0, z)
    for step in range(nz - 1):
        @pl.when((z - step >= 0) & above)
        def _(step=step):
            up(step, i - step * ny).wait_send()

        @pl.when((z + step <= nz - 1) & below)
        def _(step=step):
            down(step, i + step * ny).wait_send()

        @pl.when(z - 1 - step >= 0)
        def _(step=step):
            across_wait(1 + 2 * step, z - 1 - step)

        @pl.when(z + 1 + step <= nz - 1)
        def _(step=step):
            across_wait(2 + 2 * step, z + 1 + step)


def gathered(modal, groups, ways):
    share, times = modal.shape
    slab = times // ways
    ny = max(ways // 2, 1)
    if groups % ny:
        ny = 1
    nz = groups // ny
    vmem = pl.BlockSpec(memory_space=pltpu.VMEM)
    dma = pltpu.SemaphoreType.DMA
    steps, others = max(nz - 1, 1), max(ny - 1, 1)
    every = pl.pallas_call(
        functools.partial(gather_kernel, ny),
        out_shape=jax.ShapeDtypeStruct((groups, ways, share, slab), modal.dtype),
        in_specs=[vmem],
        out_specs=vmem,
        scratch_shapes=[
            dma, dma((ways - 1,)), dma((ways - 1,)),
            dma((steps,)), dma((steps,)), dma((steps,)), dma((steps,)),
            dma((1 + 2 * steps, others)), dma((1 + 2 * steps, others)),
        ],
        compiler_params=pltpu.CompilerParams(
            collective_id=1, has_side_effects=True, vmem_limit_bytes=32 << 20
        ),
    )(modal)
    return every.reshape(groups * ways * share, slab)


def recover_kernel(g_ref, s_ref, m_ref, a_ref, o_ref):
    hot = lax.broadcasted_iota(jnp.int32, (g_ref.shape[0], a_ref.shape[0]), 1) == g_ref[...]
    ground = jnp.dot(hot.astype(F32).astype(BF16), a_ref[...], preferred_element_type=F32)
    summed = jnp.dot(s_ref[...], m_ref[...], preferred_element_type=F32)
    o_ref[...] = (summed + ground).astype(BF16)


def recovered(groups, mode_shapes, modal, support_accel):
    dofs, modes = mode_shapes.shape
    supports, slab = support_accel.shape
    tile = min(512, dofs)
    return pl.pallas_call(
        recover_kernel,
        grid=(dofs // tile,),
        out_shape=jax.ShapeDtypeStruct((dofs, slab), BF16),
        in_specs=[
            pl.BlockSpec((tile, 1), lambda i: (i, 0)),
            pl.BlockSpec((tile, modes), lambda i: (i, 0)),
            pl.BlockSpec((modes, slab), lambda i: (0, 0)),
            pl.BlockSpec((supports, slab), lambda i: (0, 0)),
        ],
        out_specs=pl.BlockSpec((tile, slab), lambda i: (i, 0)),
        compiler_params=pltpu.CompilerParams(vmem_limit_bytes=57 << 20),
    )(groups[:, None], mode_shapes, modal, support_accel)


def per_device(support_accel, participation, kernels, lengths, mode_shapes, groups):
    ways = lax.axis_size("tm")
    share = kernels.shape[0] // ways
    first = lax.axis_index("tm") * share
    forces = jnp.dot(participation, support_accel, preferred_element_type=F32)
    mine = exchanged(forces, ways)
    modal = filtered(
        mine,
        lax.dynamic_slice_in_dim(kernels, first, share, 0),
        lax.dynamic_slice_in_dim(lengths, first, share, 0),
    )
    every = gathered(modal, lax.axis_size("mode"), ways)
    return recovered(groups, mode_shapes, every, support_accel)


def solution(mesh):
    placed = (
        P(None, "tm"),
        P("mode", None),
        P("mode", None),
        P("mode"),
        P("mode", None),
        P("mode"),
    )
    return jax.shard_map(
        per_device, mesh=mesh, in_specs=placed, out_specs=P("mode", "tm"), check_vma=False
    )
```
